32 devices in a mesh: rep: 4 (over y, x), shard: 8 (over z, core).
Axes of the slice: x: 2, y: 2, z: 4, core: 2. Of those that a mesh axis runs over, the one named last changes fastest.
Arguments:
- latents_in: float32 [32, 256, 768], P(('rep', 'shard')), may hold values from -6 to 6
- conditioning: float32 [32, 768], P(('rep', 'shard')), may hold values from -6 to 6
- cotangent: float32 [32, 256, 768], P(('rep', 'shard')), may hold values from -6 to 6
- ada_weight: bfloat16 [768, 4608], P(None, 'shard'), may hold values from -0.21875 to 0.21875
- ada_bias: bfloat16 [4608], P('shard'), may hold values from -3 to 3
- qkv_weight: bfloat16 [768, 2304], P(None, 'shard'), may hold values from -0.21875 to 0.21875
- query_bias: bfloat16 [768], P('shard'), may hold values from -6 to 6
- value_bias: bfloat16 [768], P('shard'), may hold values from -6 to 6
- proj_weight: bfloat16 [768, 768], P(None, 'shard'), may hold values from -1.75 to 1.75
- proj_bias: bfloat16 [768], P('shard'), may hold values from -6 to 6
- fc1_weight: bfloat16 [768, 3072], P(None, 'shard'), may hold values from -0.21875 to 0.21875
- fc1_bias: bfloat16 [3072], P('shard'), may hold values from -6 to 6
- fc2_weight: bfloat16 [3072, 768], P(None, 'shard'), may hold values from -0.109375 to 0.109375
- fc2_bias: bfloat16 [768], P('shard'), may hold values from -6 to 6
Outputs:
- block_out: float32 [32, 256, 768], P(('rep', 'shard'))
- grad_input: float32 [32, 256, 768], P(('rep', 'shard'))
- grad_cond: float32 [32, 768], P(('rep', 'shard'))
- grad_ada_weight: float32 [768, 4608], P(None, 'shard')
- grad_ada_bias: float32 [4608], P('shard')
- grad_qkv_weight: float32 [768, 2304], P(None, 'shard')
- grad_query_bias: float32 [768], P('shard')
- grad_value_bias: float32 [768], P('shard')
- grad_proj_weight: float32 [768, 768], P(None, 'shard')
- grad_proj_bias: float32 [768], P('shard')
- grad_fc1_weight: float32 [768, 3072], P(None, 'shard')
- grad_fc1_bias: float32 [3072], P('shard')
- grad_fc2_weight: float32 [3072, 768], P(None, 'shard')
- grad_fc2_bias: float32 [768], P('shard')
The draws below stay inside these ranges and needn't reach their ends.
All inputs are finite; a program needn't handle non-finite values.
Results may differ from the reference program's by a relative error of at most 0.01.
The reference program's roundings to bfloat16 on the way count: a program that leaves them out, or rounds other values in their place, can miss the bound.
Values may be sent and summed in bfloat16 or wider, within the bound.
No kernel may reach another device: no remote copies, remote signals or barrier semaphores. Data moves between devices by JAX's collectives and lax.ppermute only.
A program may use at most 192 MiB of HBM per device.

```python
import math
import jax
import jax.numpy as jnp
from jax import lax

D = 768
HEAD = 64
FF = 3072
S = 256
LATENTS = 32


def spiked(array, stream_key, source, target, blocks, factor):
    def block_of(dim):
        return (jnp.arange(array.shape[dim]) // (array.shape[dim] // blocks)).reshape((-1,) + (1,) * (array.ndim - 1 - dim))

    one_side = jax.random.permutation(stream_key, blocks)[block_of(target)]
    other_side = (block_of(target) + blocks // 2) % blocks
    return jnp.where((block_of(source) == one_side) | (block_of(source) == other_side), factor * array, array)


def level_of(stream_key, dims, pieces, low, largest):
    loudness = 1.0
    for dim, shards_of in pieces:
        steps = jax.random.uniform(jax.random.fold_in(jax.random.fold_in(stream_key, 6), dim), (shards_of,), jnp.float32, low / len(pieces), largest / len(pieces))
        loudness = loudness * jnp.repeat(jnp.exp(steps), dims[dim] // shards_of).reshape((-1,) + (1,) * (len(dims) - 1 - dim))
    return loudness


def normal_values(stream_key, dims, spread, bound, pieces=(), dtype=jnp.bfloat16):
    level = level_of(stream_key, dims, pieces, -0.22, 0.18) if pieces else 1.0
    array = jax.random.normal(stream_key, dims, jnp.float32) * spread * level
    return jnp.minimum(jnp.maximum(array, -bound), bound).astype(dtype)


def bell_draw_with(rng, shape, scale, bound, pieces, heavy, held_as=jnp.bfloat16):
    values = scale * jax.random.normal(rng, shape, jnp.float32)
    if pieces:
        values = values * level_of(rng, shape, pieces, -0.22, 0.18)
    return jnp.clip(spiked(values, jax.random.fold_in(rng, 3), *heavy), -bound, bound).astype(held_as)


def setup_inputs(seed: int = 0) -> dict:
    keys = jax.random.split(jax.random.key(seed), 15)
    latents_in = normal_values(keys[0], (LATENTS, S, D), 1.0, 6.0, ((0, 32),), jnp.float32)
    conditioning = normal_values(keys[1], (LATENTS, D), 1.0, 6.0, ((0, 32),), jnp.float32)
    cotangent = bell_draw_with(keys[2], (LATENTS, S, D), 1.0, 6.0, ((0, 32),), (0, 2, 32, 2.75), jnp.float32)
    ada_weight = normal_values(keys[3], (D, 6 * D), D ** -0.5, 0.21875, ((1, 8),))
    ada_bias = normal_values(keys[4], (6 * D,), 0.5, 3.0, ((0, 8),))
    qkv_weight = normal_values(keys[5], (D, 3 * D), D ** -0.5, 0.21875, ((1, 8),))
    query_bias = normal_values(keys[6], (D,), 1.0, 6.0, ((0, 8),))
    value_bias = normal_values(keys[7], (D,), 1.0, 6.0, ((0, 8),))
    proj_weight = normal_values(keys[8], (D, D), (D // 64) ** -0.5, 1.75, ((1, 8),))
    proj_bias = normal_values(keys[9], (D,), 1.0, 6.0, ((0, 8),))
    fc1_weight = normal_values(keys[10], (D, FF), D ** -0.5, 0.21875, ((1, 8),))
    fc1_bias = normal_values(keys[11], (FF,), 1.0, 6.0, ((0, 8),))
    fc2_weight = normal_values(keys[12], (FF, D), FF ** -0.5, 0.109375, ((1, 8),))
    fc2_bias = normal_values(keys[13], (D,), 1.0, 6.0, ((0, 8),))
    return {"latents_in": latents_in, "conditioning": conditioning, "cotangent": cotangent, "ada_weight": ada_weight, "ada_bias": ada_bias, "qkv_weight": qkv_weight, "query_bias": query_bias, "value_bias": value_bias, "proj_weight": proj_weight, "proj_bias": proj_bias, "fc1_weight": fc1_weight, "fc1_bias": fc1_bias, "fc2_weight": fc2_weight, "fc2_bias": fc2_bias}


gelu_scale = math.sqrt(2.0 / math.pi)
gelu_cubic = 0.044715
norm_eps = 1e-06

def layer_norm(values):
    center = values - lax.optimization_barrier(jnp.mean(values, axis=-1, keepdims=True))
    variance = lax.optimization_barrier(jnp.mean(center * center, axis=-1, keepdims=True))
    inv_std = lax.rsqrt(variance + norm_eps)
    return (center * inv_std, inv_std)

def norm_back(grad_normed, normed, inv_std):
    return inv_std * (grad_normed - lax.optimization_barrier(jnp.mean(grad_normed, axis=-1, keepdims=True)) - normed * lax.optimization_barrier(jnp.mean(grad_normed * normed, axis=-1, keepdims=True)))

def head_product(form, left, right):
    return jnp.einsum(form, left.astype(jnp.float32), right.astype(jnp.float32))

def attn_scores(query_heads, key_heads):
    return head_product('qhd,khd->hqk', query_heads, key_heads) * HEAD ** (-0.5)

def forward_latent(latent, cond_vec, weights):
    ada_weight, ada_bias, qkv_weight, query_bias, value_bias, proj_weight, proj_bias, fc1_weight, fc1_bias, fc2_weight, fc2_bias = weights
    width = latent.shape[-1]
    seq_len = latent.shape[0]
    head_count = width // HEAD
    cond_row = cond_vec[None, :]
    sigmoid_c = jax.nn.sigmoid(cond_row)
    cond_act = (cond_row * sigmoid_c).astype(jnp.bfloat16)
    modulation = jnp.dot(cond_act, ada_weight, preferred_element_type=jnp.float32) + ada_bias.astype(jnp.float32)
    shift_one, scale_one, gate_one, shift_two, scale_two, gate_two = jnp.split(modulation, 6, axis=1)
    normed_one, inv_one = layer_norm(latent)
    hidden_one = (normed_one * (1.0 + scale_one) + shift_one).astype(jnp.bfloat16)
    qkv_rows = jnp.dot(hidden_one, qkv_weight, preferred_element_type=jnp.float32)
    query_heads = (qkv_rows[:, :width] + query_bias.astype(jnp.float32)).astype(jnp.bfloat16).reshape(seq_len, head_count, HEAD)
    key_heads = qkv_rows[:, width:2 * width].astype(jnp.bfloat16).reshape(seq_len, head_count, HEAD)
    value_heads = (qkv_rows[:, 2 * width:] + value_bias.astype(jnp.float32)).astype(jnp.bfloat16).reshape(seq_len, head_count, HEAD)
    scores = attn_scores(query_heads, key_heads)
    row_max = lax.optimization_barrier(jnp.max(scores, axis=-1, keepdims=True))
    log_total = row_max + jnp.log(lax.optimization_barrier(jnp.sum(jnp.exp(scores - row_max), axis=-1, keepdims=True)))
    prob_low = jnp.exp(scores - log_total).astype(jnp.bfloat16)
    attended = head_product('hqk,khd->qhd', prob_low, value_heads).reshape(seq_len, width).astype(jnp.bfloat16)
    attn_out = jnp.dot(attended, proj_weight, preferred_element_type=jnp.float32) + proj_bias.astype(jnp.float32)
    resid_mid = latent + gate_one * attn_out
    normed_two, inv_two = layer_norm(resid_mid)
    hidden_two = (normed_two * (1.0 + scale_two) + shift_two).astype(jnp.bfloat16)
    fc1_pre = jnp.dot(hidden_two, fc1_weight, preferred_element_type=jnp.float32) + fc1_bias.astype(jnp.float32)
    tanh_inner = jnp.tanh(gelu_scale * (fc1_pre + gelu_cubic * fc1_pre * fc1_pre * fc1_pre))
    fc1_act = (0.5 * fc1_pre * (1.0 + tanh_inner)).astype(jnp.bfloat16)
    mlp_out = jnp.dot(fc1_act, fc2_weight, preferred_element_type=jnp.float32) + fc2_bias.astype(jnp.float32)
    block_out = resid_mid + gate_two * mlp_out
    saved = (cond_row, sigmoid_c, cond_act, modulation, normed_one, inv_one, hidden_one, query_heads, key_heads, value_heads, log_total, attended, attn_out, normed_two, inv_two, hidden_two, fc1_pre, tanh_inner, fc1_act, mlp_out)
    return (block_out, saved)

def backward_latent(cotangent, saved, weights, arrange):
    ada_weight, ada_bias, qkv_weight, query_bias, value_bias, proj_weight, proj_bias, fc1_weight, fc1_bias, fc2_weight, fc2_bias = weights
    cond_row, sigmoid_c, cond_act, modulation, normed_one, inv_one, hidden_one, query_heads, key_heads, value_heads, log_total, attended, attn_out, normed_two, inv_two, hidden_two, fc1_pre, tanh_inner, fc1_act, mlp_out = saved
    seq_len, width = attended.shape
    shift_one, scale_one, gate_one, shift_two, scale_two, gate_two = jnp.split(modulation, 6, axis=1)
    grad_gate_two = lax.optimization_barrier(jnp.sum(cotangent * mlp_out, axis=0, keepdims=True))
    grad_mlp = cotangent * gate_two
    grad_mlp_low = grad_mlp.astype(jnp.bfloat16)
    grad_fc2_bias = lax.optimization_barrier(jnp.sum(grad_mlp, axis=0))
    grad_fc2 = jnp.dot(fc1_act.T, arrange(grad_mlp_low), preferred_element_type=jnp.float32)
    grad_act = jnp.dot(grad_mlp_low, fc2_weight.T, preferred_element_type=jnp.float32)
    slope = 0.5 * (1.0 + tanh_inner) + 0.5 * fc1_pre * (1.0 - tanh_inner * tanh_inner) * gelu_scale * (1.0 + 3.0 * gelu_cubic * fc1_pre * fc1_pre)
    grad_pre = grad_act * slope
    grad_pre_low = grad_pre.astype(jnp.bfloat16)
    grad_fc1_bias = lax.optimization_barrier(jnp.sum(grad_pre, axis=0))
    grad_fc1 = jnp.dot(hidden_two.T, arrange(grad_pre_low), preferred_element_type=jnp.float32)
    grad_hidden_two = jnp.dot(grad_pre_low, fc1_weight.T, preferred_element_type=jnp.float32)
    grad_shift_two = lax.optimization_barrier(jnp.sum(grad_hidden_two, axis=0, keepdims=True))
    grad_scale_two = lax.optimization_barrier(jnp.sum(grad_hidden_two * normed_two, axis=0, keepdims=True))
    grad_mid = cotangent + norm_back(grad_hidden_two * (1.0 + scale_two), normed_two, inv_two)
    grad_gate_one = lax.optimization_barrier(jnp.sum(grad_mid * attn_out, axis=0, keepdims=True))
    grad_attn = grad_mid * gate_one
    grad_attn_low = grad_attn.astype(jnp.bfloat16)
    grad_proj_bias = lax.optimization_barrier(jnp.sum(grad_attn, axis=0))
    grad_proj = jnp.dot(attended.T, arrange(grad_attn_low), preferred_element_type=jnp.float32)
    head_count = width // HEAD
    grad_attended = jnp.dot(grad_attn_low, proj_weight.T, preferred_element_type=jnp.float32).astype(jnp.bfloat16).reshape(seq_len, head_count, HEAD)
    scores = attn_scores(query_heads, key_heads)
    prob_full = jnp.exp(scores - log_total)
    prob_low = prob_full.astype(jnp.bfloat16)
    grad_value = head_product('hqk,qhd->khd', prob_low, grad_attended).reshape(seq_len, width)
    grad_prob = head_product('qhd,khd->hqk', grad_attended, value_heads)
    row_delta = lax.optimization_barrier(jnp.sum(prob_full * grad_prob, axis=-1, keepdims=True))
    grad_scores = (prob_full * (grad_prob - row_delta) * HEAD ** (-0.5)).astype(jnp.bfloat16)
    grad_query = head_product('hqk,khd->qhd', grad_scores, key_heads).reshape(seq_len, width)
    grad_key = head_product('hqk,qhd->khd', grad_scores, query_heads).reshape(seq_len, width)
    grad_query_bias = lax.optimization_barrier(jnp.sum(grad_query, axis=0))
    grad_value_bias = lax.optimization_barrier(jnp.sum(grad_value, axis=0))
    grad_qkv_low = jnp.concatenate([grad_query, grad_key, grad_value], axis=1).astype(jnp.bfloat16)
    grad_qkv = jnp.dot(hidden_one.T, arrange(grad_qkv_low), preferred_element_type=jnp.float32)
    grad_hidden_one = jnp.dot(grad_qkv_low, qkv_weight.T, preferred_element_type=jnp.float32)
    grad_shift_one = lax.optimization_barrier(jnp.sum(grad_hidden_one, axis=0, keepdims=True))
    grad_scale_one = lax.optimization_barrier(jnp.sum(grad_hidden_one * normed_one, axis=0, keepdims=True))
    grad_latent = grad_mid + norm_back(grad_hidden_one * (1.0 + scale_one), normed_one, inv_one)
    grad_mod = jnp.concatenate([grad_shift_one, grad_scale_one, grad_gate_one, grad_shift_two, grad_scale_two, grad_gate_two], axis=1)
    grad_mod_low = grad_mod.astype(jnp.bfloat16)
    grad_ada = jnp.dot(cond_act.T, arrange(grad_mod_low), preferred_element_type=jnp.float32)
    grad_cond_row = jnp.dot(grad_mod_low, ada_weight.T, preferred_element_type=jnp.float32)
    grad_cond = (grad_cond_row * sigmoid_c * (1.0 + cond_row * (1.0 - sigmoid_c)))[0]
    grads = (grad_ada, arrange(grad_mod[0]), grad_qkv, arrange(grad_query_bias), arrange(grad_value_bias), grad_proj, arrange(grad_proj_bias), grad_fc1, arrange(grad_fc1_bias), grad_fc2, arrange(grad_fc2_bias))
    return (grad_latent, grad_cond, grads)

def keep_order(values):
    return values

def reference(latents_in, conditioning, cotangent, ada_weight, ada_bias, qkv_weight, query_bias, value_bias, proj_weight, proj_bias, fc1_weight, fc1_bias, fc2_weight, fc2_bias):
    weights = (ada_weight, ada_bias, qkv_weight, query_bias, value_bias, proj_weight, proj_bias, fc1_weight, fc1_bias, fc2_weight, fc2_bias)

    def step(totals, items):
        latent, cond_vec, cot_rows = items
        block_out, saved = forward_latent(latent, cond_vec, weights)
        grad_latent, grad_cond, grads = backward_latent(cot_rows, saved, weights, keep_order)
        totals = tuple((total + grad for total, grad in zip(totals, grads)))
        return (totals, (block_out, grad_latent, grad_cond))
    initial = tuple((jnp.zeros(weight.shape, jnp.float32) for weight in weights))
    totals, outputs = lax.scan(step, initial, (latents_in, conditioning, cotangent))
    return (outputs[0], outputs[1], outputs[2], totals[0], totals[1], totals[2], totals[3], totals[4], totals[5], totals[6], totals[7], totals[8], totals[9], totals[10])
```

```python
import math

import jax
import jax.numpy as jnp
from jax import lax
from jax.experimental import pallas as pl
from jax.experimental.pallas import tpu as pltpu
from jax.sharding import PartitionSpec as P

HEAD = 64
ALL = ("rep", "shard")

gelu_scale = math.sqrt(2.0 / math.pi)
gelu_cubic = 0.044715
norm_eps = 1e-06

f32 = jnp.float32
bf16 = jnp.bfloat16


def layer_norm(values):
    center = values - jnp.mean(values, axis=-1, keepdims=True)
    variance = jnp.mean(center * center, axis=-1, keepdims=True)
    inv_std = lax.rsqrt(variance + norm_eps)
    return (center * inv_std, inv_std)


def norm_back(grad_normed, normed, inv_std):
    return inv_std * (
        grad_normed
        - jnp.mean(grad_normed, axis=-1, keepdims=True)
        - normed * jnp.mean(grad_normed * normed, axis=-1, keepdims=True)
    )


def head_product(form, left, right):
    return jnp.einsum(form, left, right, preferred_element_type=f32)


def flat_rows(values):
    return values.reshape(-1, values.shape[-1])


def matmul(left, right):
    return jnp.dot(left, right, preferred_element_type=f32)


def matmul_nt(left, right):
    return lax.dot_general(left, right, (((1,), (1,)), ((), ())), preferred_element_type=f32)


def matmul_tn(left, right):
    return lax.dot_general(left, right, (((0,), (0,)), ((), ())), preferred_element_type=f32)


class Cube:
    def __init__(self, n_rep, n_shard):
        self.n_rep, self.n_shard = n_rep, n_shard
        self.rep_bits = n_rep.bit_length() - 1
        self.shard_bits = n_shard.bit_length() - 1
        self.rep = lax.axis_index("rep")
        self.shard = lax.axis_index("shard")

    def swap(self, values, mask):
        total = self.n_rep * self.n_shard
        return lax.ppermute(values, ALL, [(i, i ^ mask) for i in range(total)])

    def swap_shard(self, values, bit):
        return self.swap(values, 1 << bit)

    def swap_rep(self, values, bit):
        return self.swap(values, self.n_shard << bit)

    def shard_bit(self, bit):
        return (self.shard >> bit) & 1

    def rep_bit(self, bit):
        return (self.rep >> bit) & 1


def reorder(values, me, bits, axis=0):
    shape = values.shape
    for bit in range(bits):
        low = 1 << bit
        split = shape[:axis] + (shape[axis] // (2 * low), 2, low) + shape[axis + 1 :]
        view = values.reshape(split)
        flipped = jnp.flip(view, axis=axis + 1)
        values = jnp.where(((me >> bit) & 1) == 1, flipped, view).reshape(shape)
    return values


def pick(values, bit, axis):
    return lax.dynamic_index_in_dim(values, bit, axis, keepdims=False)


def small_gather(cube, row):
    for bit in range(cube.shard_bits):
        row = jnp.concatenate([row, cube.swap_shard(row, bit)], axis=0)
    return row


def small_gather_rep(cube, rows):
    for bit in range(cube.rep_bits):
        rows = jnp.concatenate([rows, cube.swap_rep(rows, bit)], axis=0)
    return rows


def small_exchange(cube, rows):
    shape = rows.shape
    for bit in reversed(range(cube.shard_bits)):
        low = 1 << bit
        view = rows.reshape((shape[0] // (2 * low), 2, low) + shape[1:])
        other = cube.swap_shard(view[:, 1], bit)
        rows = jnp.stack([view[:, 0], other], axis=1).reshape(shape)
    return rows


def small_scatter_sum(cube, rows):
    for bit in reversed(range(cube.shard_bits)):
        half = rows.shape[0] // 2
        rows = rows[:half] + cube.swap_shard(rows[half:], bit)
    return rows


def assemble_kernel(cube_sizes, names, *refs):
    n_rep, n_shard = cube_sizes
    out_ref, sems = refs[-2], refs[-1]
    rep = lax.axis_index("rep")
    shard = lax.axis_index("shard")
    copies = []
    for ref, name in zip(refs[:-2], names):
        if name[0] == "whole":
            target = jnp.bitwise_xor(shard, name[1])
            copies.append((ref, out_ref.at[target]))
        else:
            _, core, part, steps = name
            for place, step in enumerate(steps):
                target = jnp.bitwise_xor(shard, 2 * step + core)
                copies.append((ref.at[place], out_ref.at[target, jnp.bitwise_xor(rep, part)]))
    started = [
        pltpu.make_async_copy(source, target, sems.at[k]) for k, (source, target) in enumerate(copies)
    ]
    for copy in started:
        copy.start()
    for copy in started:
        copy.wait()


def gather_weight(cube, shard_rows):
    rows, width = shard_rows.shape
    parts = cube.n_rep
    own = shard_rows.reshape(parts, rows // parts, width)
    partner = cube.swap_shard(own, 0)
    mine = pick(own, cube.rep, 0)[None]
    gathered = mine
    for bit in range(1, cube.shard_bits):
        gathered = jnp.concatenate([gathered, cube.swap_shard(gathered, bit)], axis=0)
    steps = tuple(range(1, cube.n_shard // 2))
    gathered = gathered[1:]
    pieces = [(0, steps, gathered)]
    if cube.rep_bits == 2:
        via_x = cube.swap_rep(gathered, 0)
        via_y = cube.swap_rep(gathered, 1)
        cut = len(steps) // 2
        far_x = cube.swap_rep(via_y[:cut], 0)
        far_y = cube.swap_rep(via_x[cut:], 1)
        pieces += [(1, steps, via_x), (2, steps, via_y), (3, steps[:cut], far_x), (3, steps[cut:], far_y)]
    else:
        for bit in range(cube.rep_bits):
            pieces += [
                (part | (1 << bit), held, cube.swap_rep(values, bit)) for part, held, values in pieces
            ]
    operands, names = [own, partner], [("whole", 0), ("whole", 1)]
    for part, held, values in pieces:
        operands.append(values)
        names.append(("piece", 0, part, held))
    for part, held, values in pieces:
        operands.append(cube.swap_shard(values, 0))
        names.append(("piece", 1, part, held))
    copies = sum(1 if name[0] == "whole" else len(name[3]) for name in names)

    def body(*refs):
        assemble_kernel((cube.n_rep, cube.n_shard), names, *refs)

    return pl.pallas_call(
        body,
        out_shape=jax.ShapeDtypeStruct((cube.n_shard,) + own.shape, own.dtype),
        in_specs=[pl.BlockSpec(memory_space=pl.ANY)] * len(operands),
        out_specs=pl.BlockSpec(memory_space=pltpu.VMEM),
        scratch_shapes=[pltpu.SemaphoreType.DMA((copies,))],
        name="assemble",
    )(*operands)


def reduce_grad(cube, grad):
    q, width = grad.shape[2:]
    zs = cube.shard_bits - 1
    view = grad.reshape((2,) * (zs + 1 + cube.rep_bits) + (q, width))

    def halve(values, axis, bit, swap):
        keep = pick(values, bit, axis)
        send = pick(values, 1 - bit, axis).astype(bf16)
        return keep + swap(send).astype(f32)

    view = halve(view, zs, cube.shard_bit(0), lambda v: cube.swap_shard(v, 0))
    rep_axes = list(range(zs, zs + cube.rep_bits))

    def halve_rep(values, order, base):
        left = list(range(cube.rep_bits - 1, -1, -1))
        for bit in order:
            axis = base + left.index(bit)
            left.remove(bit)
            values = halve(values, axis, cube.rep_bit(bit), lambda v, bit=bit: cube.swap_rep(v, bit))
        return values

    if cube.rep_bits == 2:
        view = jnp.stack(
            [halve_rep(view[0], (0, 1), zs - 1), halve_rep(view[1], (1, 0), zs - 1)], axis=0
        )
    else:
        view = halve_rep(view, tuple(range(cube.rep_bits)), zs)
    for bit in range(cube.shard_bits - 1, 0, -1):
        view = halve(view, 0, cube.shard_bit(bit), lambda v, bit=bit: cube.swap_shard(v, bit))
    return view


def spread_parts(cube, part):
    part = lax.optimization_barrier(part.astype(bf16))
    if cube.rep_bits == 2:
        half = part.shape[1] // 2
        via_x = cube.swap_rep(part, 0)
        via_y = cube.swap_rep(part, 1)
        far = jnp.concatenate(
            [cube.swap_rep(via_y[:, :half], 0), cube.swap_rep(via_x[:, half:], 1)], axis=1
        )
        parts = jnp.stack([part, via_x, via_y, far])
    else:
        parts = part[None]
        for bit in range(cube.rep_bits):
            parts = jnp.concatenate([parts, cube.swap_rep(parts, bit)], axis=0)
    return reorder(parts, cube.rep, cube.rep_bits)


def forward_all(latents, modulation, weights):
    qkv_weight, query_bias, value_bias, proj_weight, proj_bias, fc1_weight, fc1_bias, fc2_weight, fc2_bias = weights
    count, seq_len, width = latents.shape
    head_count = width // HEAD
    mods = [piece[:, None, :] for piece in jnp.split(modulation, 6, axis=1)]
    shift_one, scale_one, gate_one, shift_two, scale_two, gate_two = mods
    normed_one, inv_one = layer_norm(latents)
    hidden_one = (normed_one * (1.0 + scale_one) + shift_one).astype(bf16)
    qkv_rows = matmul_nt(flat_rows(hidden_one), qkv_weight)
    head_shape = (count, seq_len, head_count, HEAD)
    query_heads = (
        (qkv_rows[:, :width] + query_bias.astype(f32)).astype(bf16).reshape(head_shape)
    )
    key_heads = qkv_rows[:, width : 2 * width].astype(bf16).reshape(head_shape)
    value_heads = (
        (qkv_rows[:, 2 * width :] + value_bias.astype(f32)).astype(bf16).reshape(head_shape)
    )
    scores = head_product("lqhd,lkhd->lhqk", query_heads, key_heads) * HEAD ** (-0.5)
    row_max = jnp.max(scores, axis=-1, keepdims=True)
    log_total = row_max + jnp.log(jnp.sum(jnp.exp(scores - row_max), axis=-1, keepdims=True))
    prob_low = jnp.exp(scores - log_total).astype(bf16)
    attended = (
        head_product("lhqk,lkhd->lqhd", prob_low, value_heads)
        .reshape(count, seq_len, width)
        .astype(bf16)
    )
    attn_out = (matmul_nt(flat_rows(attended), proj_weight) + proj_bias.astype(f32)).reshape(
        count, seq_len, width
    )
    resid_mid = latents + gate_one * attn_out
    normed_two, inv_two = layer_norm(resid_mid)
    hidden_two = (normed_two * (1.0 + scale_two) + shift_two).astype(bf16)
    fc1_pre = (matmul_nt(flat_rows(hidden_two), fc1_weight) + fc1_bias.astype(f32)).reshape(
        count, seq_len, -1
    )
    tanh_inner = jnp.tanh(gelu_scale * (fc1_pre + gelu_cubic * fc1_pre * fc1_pre * fc1_pre))
    fc1_act = (0.5 * fc1_pre * (1.0 + tanh_inner)).astype(bf16)
    mlp_out = (matmul_nt(flat_rows(fc1_act), fc2_weight) + fc2_bias.astype(f32)).reshape(
        count, seq_len, width
    )
    block_out = resid_mid + gate_two * mlp_out
    saved = (
        modulation, normed_one, inv_one, hidden_one, query_heads, key_heads, value_heads, log_total,
        attended, attn_out, normed_two, inv_two, hidden_two, fc1_pre, tanh_inner, fc1_act, mlp_out,
    )
    return (block_out, saved)


def backward_all(cotangent, saved, weights):
    qkv_weight, _, _, proj_weight, _, fc1_weight, _, fc2_weight, _ = weights
    (
        modulation, normed_one, inv_one, hidden_one, query_heads, key_heads, value_heads, log_total,
        attended, attn_out, normed_two, inv_two, hidden_two, fc1_pre, tanh_inner, fc1_act, mlp_out,
    ) = saved
    count, seq_len, width = attended.shape
    head_count = width // HEAD
    mods = [piece[:, None, :] for piece in jnp.split(modulation, 6, axis=1)]
    shift_one, scale_one, gate_one, shift_two, scale_two, gate_two = mods
    grad_gate_two = jnp.sum(cotangent * mlp_out, axis=1)
    grad_mlp = cotangent * gate_two
    grad_mlp_low = flat_rows(grad_mlp.astype(bf16))
    grad_fc2_bias = jnp.sum(flat_rows(grad_mlp), axis=0)
    grad_fc2 = matmul_tn(grad_mlp_low, flat_rows(fc1_act))
    grad_act = matmul(grad_mlp_low, fc2_weight).reshape(fc1_pre.shape)
    slope = 0.5 * (1.0 + tanh_inner) + 0.5 * fc1_pre * (
        1.0 - tanh_inner * tanh_inner
    ) * gelu_scale * (1.0 + 3.0 * gelu_cubic * fc1_pre * fc1_pre)
    grad_pre = grad_act * slope
    grad_pre_low = flat_rows(grad_pre.astype(bf16))
    grad_fc1_bias = jnp.sum(flat_rows(grad_pre), axis=0)
    grad_fc1 = matmul_tn(grad_pre_low, flat_rows(hidden_two))
    grad_hidden_two = matmul(grad_pre_low, fc1_weight).reshape(count, seq_len, width)
    grad_shift_two = jnp.sum(grad_hidden_two, axis=1)
    grad_scale_two = jnp.sum(grad_hidden_two * normed_two, axis=1)
    grad_mid = cotangent + norm_back(grad_hidden_two * (1.0 + scale_two), normed_two, inv_two)
    grad_gate_one = jnp.sum(grad_mid * attn_out, axis=1)
    grad_attn = grad_mid * gate_one
    grad_attn_low = flat_rows(grad_attn.astype(bf16))
    grad_proj_bias = jnp.sum(flat_rows(grad_attn), axis=0)
    grad_proj = matmul_tn(grad_attn_low, flat_rows(attended))
    head_shape = (count, seq_len, head_count, HEAD)
    grad_attended = matmul(grad_attn_low, proj_weight).astype(bf16).reshape(head_shape)
    scores = head_product("lqhd,lkhd->lhqk", query_heads, key_heads) * HEAD ** (-0.5)
    prob_full = jnp.exp(scores - log_total)
    prob_low = prob_full.astype(bf16)
    grad_value = head_product("lhqk,lqhd->lkhd", prob_low, grad_attended).reshape(
        count * seq_len, width
    )
    grad_prob = head_product("lqhd,lkhd->lhqk", grad_attended, value_heads)
    row_delta = jnp.sum(prob_full * grad_prob, axis=-1, keepdims=True)
    grad_scores = (prob_full * (grad_prob - row_delta) * HEAD ** (-0.5)).astype(bf16)
    grad_query = head_product("lhqk,lkhd->lqhd", grad_scores, key_heads).reshape(
        count * seq_len, width
    )
    grad_key = head_product("lhqk,lqhd->lkhd", grad_scores, query_heads).reshape(
        count * seq_len, width
    )
    grad_query_bias = jnp.sum(grad_query, axis=0)
    grad_value_bias = jnp.sum(grad_value, axis=0)
    grad_qkv_low = jnp.concatenate([grad_query, grad_key, grad_value], axis=1).astype(bf16)
    grad_qkv = matmul_tn(grad_qkv_low, flat_rows(hidden_one))
    grad_hidden_one = matmul(grad_qkv_low, qkv_weight).reshape(count, seq_len, width)
    grad_shift_one = jnp.sum(grad_hidden_one, axis=1)
    grad_scale_one = jnp.sum(grad_hidden_one * normed_one, axis=1)
    grad_latent = grad_mid + norm_back(grad_hidden_one * (1.0 + scale_one), normed_one, inv_one)
    grad_mod = jnp.concatenate(
        [grad_shift_one, grad_scale_one, grad_gate_one, grad_shift_two, grad_scale_two, grad_gate_two],
        axis=1,
    )
    biases = (grad_query_bias, grad_value_bias, grad_proj_bias, grad_fc1_bias, grad_fc2_bias)
    return (grad_latent, grad_mod, biases, grad_qkv, grad_proj, grad_fc1, grad_fc2)


def local_step(
    cube,
    latents_in,
    conditioning,
    cotangent,
    ada_weight,
    ada_bias,
    qkv_weight,
    query_bias,
    value_bias,
    proj_weight,
    proj_bias,
    fc1_weight,
    fc1_bias,
    fc2_weight,
    fc2_bias,
):
    count, _, width = latents_in.shape
    n_shard, n_rep = cube.n_shard, cube.n_rep
    blocks = fc2_weight.shape[0] // width
    outs = fc2_weight.shape[1]
    wide = ada_weight.shape[1]

    sigmoid_c = jax.nn.sigmoid(conditioning)
    cond_act = (conditioning * sigmoid_c).astype(bf16)
    bias_sizes = [b.shape[0] for b in (query_bias, value_bias, proj_bias, fc1_bias, fc2_bias)]
    bias_row = jnp.concatenate([query_bias, value_bias, proj_bias, fc1_bias, fc2_bias])
    packet = jnp.concatenate([cond_act.reshape(1, -1), bias_row.reshape(1, -1)], axis=1)
    packets = small_gather(cube, packet)
    cond_group = packets[:, : count * width].reshape(n_shard * count, width)
    bias_rows = reorder(packets[:, count * width :], cube.shard, cube.shard_bits)
    ends = [sum(bias_sizes[: k + 1]) for k in range(len(bias_sizes) - 1)]
    full_biases = [piece.reshape(-1) for piece in jnp.split(bias_rows, ends, axis=1)]
    mod_columns = matmul(cond_group, ada_weight) + ada_bias.astype(f32)
    mod_rows = small_exchange(cube, mod_columns.reshape(n_shard, count, wide))
    mod_rows = reorder(mod_rows, cube.shard, cube.shard_bits)
    modulation = jnp.swapaxes(mod_rows, 0, 1).reshape(count, n_shard * wide)

    fc2_rows = jnp.swapaxes(fc2_weight.reshape(blocks, width, outs), 1, 2).reshape(blocks * outs, width)
    qkv_full = gather_weight(cube, qkv_weight.T).reshape(-1, width)
    proj_full = gather_weight(cube, proj_weight.T).reshape(-1, width)
    fc1_full = gather_weight(cube, fc1_weight.T).reshape(-1, width)
    fc2_full = gather_weight(cube, fc2_rows).reshape(n_shard, blocks, outs, width)
    fc2_full = jnp.swapaxes(fc2_full, 1, 2).reshape(n_shard * outs, blocks * width)
    q_bias, v_bias, p_bias, f1_bias, f2_bias = full_biases
    weights = (qkv_full, q_bias, v_bias, proj_full, p_bias, fc1_full, f1_bias, fc2_full, f2_bias)

    block_out, saved = forward_all(latents_in, modulation, weights)
    grad_input, grad_mod, biases, grad_qkv, grad_proj, grad_fc1, grad_fc2 = backward_all(
        cotangent, saved, weights
    )

    def owner_part(grad):
        rows = grad.shape[0] // (n_shard * n_rep)
        return reduce_grad(cube, grad.reshape(n_shard, n_rep, rows, width))

    grad_fc2 = jnp.swapaxes(grad_fc2.reshape(n_shard, outs, blocks, width), 1, 2)
    part_fc2 = owner_part(grad_fc2.reshape(-1, width))
    part_fc1 = owner_part(grad_fc1)
    part_proj = owner_part(grad_proj)
    part_qkv = owner_part(grad_qkv)

    early = spread_parts(cube, jnp.concatenate([part_fc2, part_fc1, part_proj], axis=0))
    late = spread_parts(cube, part_qkv)
    sizes = [part_fc2.shape[0], part_fc1.shape[0]]
    fc2_low, fc1_low, proj_low = jnp.split(early, [sizes[0], sizes[0] + sizes[1]], axis=1)
    out_qkv = late.reshape(-1, width).T.astype(f32)
    out_proj = proj_low.reshape(-1, width).T.astype(f32)
    out_fc1 = fc1_low.reshape(-1, width).T.astype(f32)
    out_fc2 = jnp.swapaxes(fc2_low.reshape(blocks, outs, width), 1, 2).reshape(blocks * width, outs)
    out_fc2 = out_fc2.astype(f32)

    per_owner = [grad_mod.reshape(count, n_shard, wide).swapaxes(0, 1).reshape(n_shard, count * wide)]
    per_owner += [b.reshape(n_shard, -1) for b in biases]
    rows = reorder(jnp.concatenate(per_owner, axis=1), cube.shard, cube.shard_bits)
    rows = small_exchange(cube, rows)
    grad_rows = rows[:, : count * wide].reshape(n_shard * count, wide)
    all_rows = small_gather_rep(cube, rows).reshape(n_rep, n_shard, -1)
    all_rows = reorder(all_rows, cube.rep, cube.rep_bits)
    all_cond = small_gather_rep(cube, cond_group).reshape(n_rep, n_shard * count, width)
    all_cond = reorder(all_cond, cube.rep, cube.rep_bits).reshape(-1, width)
    mod_all = all_rows[:, :, : count * wide].reshape(-1, wide)
    out_ada = matmul_tn(all_cond, mod_all.astype(bf16))
    out_ada_bias = jnp.sum(mod_all, axis=0)
    sums = jnp.sum(all_rows[:, :, count * wide :].reshape(n_rep * n_shard, -1), axis=0)
    out_q, out_v, out_p, out_f1, out_f2 = jnp.split(sums, ends)
    cond_part = matmul_nt(grad_rows.astype(bf16), ada_weight).reshape(n_shard, count, width)
    grad_cond_row = small_scatter_sum(cube, cond_part)[0]
    grad_cond = grad_cond_row * sigmoid_c * (1.0 + conditioning * (1.0 - sigmoid_c))
    return (
        block_out,
        grad_input,
        grad_cond,
        out_ada,
        out_ada_bias,
        out_qkv,
        out_q,
        out_v,
        out_proj,
        out_p,
        out_fc1,
        out_f1,
        out_fc2,
        out_f2,
    )


def solution(mesh):
    def local(*args):
        return local_step(Cube(mesh.shape["rep"], mesh.shape["shard"]), *args)

    placed = (
        P(("rep", "shard"), None, None),
        P(("rep", "shard"), None),
        P(("rep", "shard"), None, None),
        P(None, "shard"),
        P("shard"),
        P(None, "shard"),
        P("shard"),
        P("shard"),
        P(None, "shard"),
        P("shard"),
        P(None, "shard"),
        P("shard"),
        P(None, "shard"),
        P("shard"),
    )
    return jax.shard_map(
        local,
        mesh=mesh,
        in_specs=placed,
        out_specs=(P(("rep", "shard"), None, None), P(("rep", "shard"), None, None), P(("rep", "shard"), None)) + placed[3:],
        check_vma=False,
    )
```

```python
import math

import jax
import jax.numpy as jnp
from jax import lax
from jax.experimental import pallas as pl
from jax.experimental.pallas import tpu as pltpu
from jax.sharding import PartitionSpec as P

HEAD = 64
ALL = ("rep", "shard")

gelu_scale = math.sqrt(2.0 / math.pi)
gelu_cubic = 0.044715
norm_eps = 1e-06

f32 = jnp.float32
bf16 = jnp.bfloat16


def layer_norm(values):
    center = values - jnp.mean(values, axis=-1, keepdims=True)
    variance = jnp.mean(center * center, axis=-1, keepdims=True)
    inv_std = lax.rsqrt(variance + norm_eps)
    return (center * inv_std, inv_std)


def norm_back(grad_normed, normed, inv_std):
    return inv_std * (
        grad_normed
        - jnp.mean(grad_normed, axis=-1, keepdims=True)
        - normed * jnp.mean(grad_normed * normed, axis=-1, keepdims=True)
    )


def head_product(form, left, right):
    return jnp.einsum(form, left, right, preferred_element_type=f32)


def flat_rows(values):
    return values.reshape(-1, values.shape[-1])


def matmul(left, right):
    return jnp.dot(left, right, preferred_element_type=f32)


def matmul_nt(left, right):
    return lax.dot_general(left, right, (((1,), (1,)), ((), ())), preferred_element_type=f32)


def matmul_tn(left, right):
    return lax.dot_general(left, right, (((0,), (0,)), ((), ())), preferred_element_type=f32)


class Cube:
    def __init__(self, n_rep, n_shard):
        self.n_rep, self.n_shard = n_rep, n_shard
        self.rep_bits = n_rep.bit_length() - 1
        self.shard_bits = n_shard.bit_length() - 1
        self.rep = lax.axis_index("rep")
        self.shard = lax.axis_index("shard")

    def swap(self, values, mask):
        total = self.n_rep * self.n_shard
        return lax.ppermute(values, ALL, [(i, i ^ mask) for i in range(total)])

    def swap_shard(self, values, mask):
        return self.swap(values, mask)

    def swap_rep(self, values, mask):
        return self.swap(values, self.n_shard * mask)

    def shard_bit(self, bit):
        return (self.shard >> bit) & 1

    def rep_bit(self, bit):
        return (self.rep >> bit) & 1


def reorder(values, me, bits, axis=0):
    shape = values.shape
    for bit in range(bits):
        low = 1 << bit
        split = shape[:axis] + (shape[axis] // (2 * low), 2, low) + shape[axis + 1 :]
        view = values.reshape(split)
        flipped = jnp.flip(view, axis=axis + 1)
        values = jnp.where(((me >> bit) & 1) == 1, flipped, view).reshape(shape)
    return values


def pick(values, bit, axis):
    return lax.dynamic_index_in_dim(values, bit, axis, keepdims=False)


def small_gather(cube, row):
    for bit in range(cube.shard_bits):
        row = jnp.concatenate([row, cube.swap_shard(row, 1 << bit)], axis=0)
    return row


def small_gather_rep(cube, rows):
    for bit in range(cube.rep_bits):
        rows = jnp.concatenate([rows, cube.swap_rep(rows, 1 << bit)], axis=0)
    return rows


def small_exchange(cube, rows):
    shape = rows.shape
    for bit in reversed(range(cube.shard_bits)):
        low = 1 << bit
        view = rows.reshape((shape[0] // (2 * low), 2, low) + shape[1:])
        other = cube.swap_shard(view[:, 1], low)
        rows = jnp.stack([view[:, 0], other], axis=1).reshape(shape)
    return rows


def small_scatter_sum(cube, rows):
    for bit in reversed(range(cube.shard_bits)):
        half = rows.shape[0] // 2
        rows = rows[:half] + cube.swap_shard(rows[half:], 1 << bit)
    return rows


def assemble_kernel(cube, names, sizes, direct, *refs):
    count = len(sizes)
    out_refs, sems = refs[-1 - count : -1], refs[-1]
    rep = lax.axis_index("rep")
    shard = lax.axis_index("shard")
    copies = []
    for ref, name in zip(refs, names):
        start = 0
        for out_ref, rows in zip(out_refs, sizes):
            mine = ref if count == 1 else ref.at[:, pl.ds(start, rows)]
            start += rows
            if name[0] == "whole":
                target = jnp.bitwise_xor(shard, name[1])
                if direct:
                    for part in range(cube.n_rep):
                        place = pl.ds(pl.multiple_of(target * rows, rows), rows)
                        copies.append((mine.at[part], out_ref.at[place, pl.ds(part * ref.shape[-1], ref.shape[-1])]))
                else:
                    copies.append((mine, out_ref.at[target]))
            else:
                _, core, part, steps = name
                for place, step in enumerate(steps):
                    target = jnp.bitwise_xor(shard, 2 * step + core)
                    where = jnp.bitwise_xor(rep, part)
                    if direct:
                        width = ref.shape[-1]
                        down = pl.ds(pl.multiple_of(target * rows, rows), rows)
                        across = pl.ds(pl.multiple_of(where * width, width), width)
                        copies.append((mine.at[place], out_ref.at[down, across]))
                    else:
                        copies.append((mine.at[place], out_ref.at[target, where]))
    started = [
        pltpu.make_async_copy(source, target, sems.at[k]) for k, (source, target) in enumerate(copies)
    ]
    for copy in started:
        copy.start()
    for copy in started:
        copy.wait()


def start_gather(cube, shard_rows):
    rows, width = shard_rows.shape
    own = shard_rows.reshape(cube.n_rep, rows // cube.n_rep, width)
    mine = pick(own, cube.rep, 0)
    if cube.n_shard == 8:
        gathered = [cube.swap_shard(mine, 2 * j)[None] for j in (1, 2, 3)]
        gathered = jnp.concatenate(gathered, axis=0)
    else:
        gathered = mine[None]
        for bit in range(1, cube.shard_bits):
            other = cube.swap_shard(gathered, 1 << bit)
            gathered = jnp.concatenate([gathered, other], axis=0)
        gathered = gathered[1:]
    return own, gathered


def finish_gather(cube, own, gathered, sizes, blocks=0):
    width = own.shape[-1]
    steps = tuple(range(1, cube.n_shard // 2))
    pieces = [(0, gathered)]
    pieces += [(t, cube.swap_rep(gathered, t)) for t in range(1, cube.n_rep)]
    operands, names = [own, cube.swap_shard(own, 1)], [("whole", 0), ("whole", 1)]
    for part, values in pieces:
        operands += [values, cube.swap_shard(values, 1)]
        names += [("piece", 0, part, steps), ("piece", 1, part, steps)]
    direct = blocks == cube.n_rep and sizes[0] % 16 == 0
    split = all(size % 8 == 0 for size in sizes)
    held = sizes if split else (sum(sizes),)
    copies = len(held) * (len(pieces) * 2 * len(steps) + (2 * cube.n_rep if direct else 2))

    def body(*refs):
        assemble_kernel(cube, names, held, direct, *refs)

    def shape_of(rows):
        if direct:
            return (cube.n_shard * rows, cube.n_rep * width)
        return (cube.n_shard, cube.n_rep, rows, width)

    outs = pl.pallas_call(
        body,
        out_shape=[jax.ShapeDtypeStruct(shape_of(rows), own.dtype) for rows in held],
        in_specs=[pl.BlockSpec(memory_space=pl.ANY)] * len(operands),
        out_specs=[pl.BlockSpec(memory_space=pltpu.VMEM)] * len(held),
        scratch_shapes=[pltpu.SemaphoreType.DMA((copies,))],
    )(*operands)
    if not split:
        ends = [sum(sizes[: k + 1]) for k in range(len(sizes) - 1)]
        outs = jnp.split(outs[0], ends, axis=2)
    return outs


def start_reduce(cube, grad):
    view = grad.reshape((cube.n_shard // 2, 2) + grad.shape[1:])
    core = cube.shard_bit(0)
    return view, cube.swap_shard(pick(view, 1 - core, 1), 1)


def reduce_rep(cube, halves):
    core = cube.shard_bit(0)

    def both(part):
        sums = [
            pick(pick(view, core, 1), part, 1).astype(f32) + pick(other, part, 1).astype(f32)
            for view, other in halves
        ]
        return sums[0] if len(sums) == 1 else jnp.concatenate([v.astype(bf16) for v in sums], axis=1)

    sends = [both(cube.rep ^ t).astype(bf16) for t in range(1, cube.n_rep)]
    total = both(cube.rep).astype(f32)
    for t, send in enumerate(sends, 1):
        total = total + cube.swap_rep(send, t).astype(f32)
    return total


def reduce_shard(cube, values):
    place = cube.shard >> 1
    total = pick(values, place, 0).astype(f32)
    for j in range(1, cube.n_shard // 2):
        send = pick(values, place ^ j, 0).astype(bf16)
        total = total + cube.swap_shard(send, 2 * j).astype(f32)
    return total


def spread_parts(cube, part):
    part = lax.optimization_barrier(part.astype(bf16))
    parts = [part] + [cube.swap_rep(part, t) for t in range(1, cube.n_rep)]
    return reorder(jnp.stack(parts), cube.rep, cube.rep_bits)


def tie(*values):
    return lax.optimization_barrier(values)


def local_step(
    cube,
    latents_in,
    conditioning,
    cotangent,
    ada_weight,
    ada_bias,
    qkv_weight,
    query_bias,
    value_bias,
    proj_weight,
    proj_bias,
    fc1_weight,
    fc1_bias,
    fc2_weight,
    fc2_bias,
):
    count, _, width = latents_in.shape
    n_shard, n_rep = cube.n_shard, cube.n_rep
    blocks = fc2_weight.shape[0] // width
    outs = fc2_weight.shape[1]
    wide = ada_weight.shape[1]

    sigmoid_c = jax.nn.sigmoid(conditioning)
    cond_act = (conditioning * sigmoid_c).astype(bf16)
    fc2_rows = jnp.swapaxes(fc2_weight.reshape(blocks, width, outs), 1, 2).reshape(blocks * outs, width)
    proj_rows, fc1_rows = proj_weight.T, fc1_weight.T
    qkv_own, qkv_got = start_gather(cube, qkv_weight.T)
    both_own = jnp.concatenate(
        [proj_rows.reshape(n_rep, -1, width), fc1_rows.reshape(n_rep, -1, width)], axis=1
    )
    both_own, both_got = start_gather(cube, both_own.reshape(-1, width))
    fc2_own, fc2_got = start_gather(cube, fc2_rows)

    biases_in = (query_bias, value_bias, proj_bias, fc1_bias, fc2_bias)
    bias_sizes = [b.shape[0] for b in biases_in]
    wider = max(bias_sizes)
    bias_row = jnp.stack([jnp.pad(b, (0, wider - b.shape[0])) for b in biases_in])
    cond_group = small_gather(cube, cond_act.reshape(1, -1)).reshape(n_shard * count, width)
    bias_rows = reorder(small_gather(cube, bias_row[None]), cube.shard, cube.shard_bits)
    q_bias, v_bias, p_bias, f1_bias, f2_bias = [
        bias_rows[:, k, :size].reshape(-1).astype(f32) for k, size in enumerate(bias_sizes)
    ]
    ends = [sum(bias_sizes[: k + 1]) for k in range(len(bias_sizes) - 1)]
    mod_columns = matmul(cond_group, ada_weight) + ada_bias.astype(f32)
    mod_rows = small_exchange(cube, mod_columns.reshape(n_shard, count, wide))
    mod_rows = reorder(mod_rows, cube.shard, cube.shard_bits)
    modulation = jnp.swapaxes(mod_rows, 0, 1).reshape(count, n_shard * wide)

    (qkv_full,) = finish_gather(cube, qkv_own, qkv_got, (qkv_own.shape[1],))
    qkv_full = qkv_full.reshape(-1, width)
    proj_full, fc1_full = finish_gather(
        cube, both_own, both_got, (proj_rows.shape[0] // n_rep, fc1_rows.shape[0] // n_rep)
    )
    proj_full, fc1_full = proj_full.reshape(-1, width), fc1_full.reshape(-1, width)
    (fc2_full,) = finish_gather(cube, fc2_own, fc2_got, (fc2_own.shape[1],), blocks)
    if fc2_full.ndim == 4:
        fc2_full = jnp.swapaxes(fc2_full.reshape(n_shard, blocks, outs, width), 1, 2)
        fc2_full = fc2_full.reshape(n_shard * outs, blocks * width)

    def by_owner(grad):
        return grad.astype(bf16).reshape(n_shard, n_rep, -1, width)

    seq_len = latents_in.shape[1]
    head_count = width // HEAD
    head_shape = (count, seq_len, head_count, HEAD)
    scale = HEAD ** (-0.5)
    mods = [piece[:, None, :] for piece in jnp.split(modulation, 6, axis=1)]
    shift_one, scale_one, gate_one, shift_two, scale_two, gate_two = mods
    normed_one, inv_one = layer_norm(latents_in)
    hidden_one = (normed_one * (1.0 + scale_one) + shift_one).astype(bf16)
    qkv_rows = matmul_nt(flat_rows(hidden_one), qkv_full)
    query_heads = (qkv_rows[:, :width] + q_bias).astype(bf16).reshape(head_shape)
    key_heads = qkv_rows[:, width : 2 * width].astype(bf16).reshape(head_shape)
    value_heads = (qkv_rows[:, 2 * width :] + v_bias).astype(bf16).reshape(head_shape)
    scores = head_product("lqhd,lkhd->lhqk", query_heads, key_heads) * scale
    row_max = jnp.max(scores, axis=-1, keepdims=True)
    log_total = row_max + jnp.log(jnp.sum(jnp.exp(scores - row_max), axis=-1, keepdims=True))
    prob_low = jnp.exp(scores - log_total).astype(bf16)
    attended = (
        head_product("lhqk,lkhd->lqhd", prob_low, value_heads)
        .reshape(count, seq_len, width)
        .astype(bf16)
    )
    attn_out = (matmul_nt(flat_rows(attended), proj_full) + p_bias).reshape(count, seq_len, width)
    resid_mid = latents_in + gate_one * attn_out
    normed_two, inv_two = layer_norm(resid_mid)
    hidden_two = (normed_two * (1.0 + scale_two) + shift_two).astype(bf16)
    fc1_pre = (matmul_nt(flat_rows(hidden_two), fc1_full) + f1_bias).reshape(count, seq_len, -1)
    tanh_inner = jnp.tanh(gelu_scale * (fc1_pre + gelu_cubic * fc1_pre * fc1_pre * fc1_pre))
    fc1_act = (0.5 * fc1_pre * (1.0 + tanh_inner)).astype(bf16)

    grad_mlp = cotangent * gate_two
    grad_mlp_low = flat_rows(grad_mlp.astype(bf16))
    grad_fc2_bias = jnp.sum(flat_rows(grad_mlp), axis=0)
    act_rows = flat_rows(fc1_act)
    grad_fc2 = jnp.stack(
        [
            matmul_tn(grad_mlp_low, act_rows[:, b * width : (b + 1) * width])
            .astype(bf16)
            .reshape(n_shard, outs, width)
            for b in range(blocks)
        ],
        axis=1,
    )
    grad_fc2, fc1_act, grad_mlp_low = tie(by_owner(grad_fc2), fc1_act, grad_mlp_low)
    part_fc2 = reduce_rep(cube, [start_reduce(cube, grad_fc2)])
    mlp_out = (matmul_nt(flat_rows(fc1_act), fc2_full) + f2_bias).reshape(count, seq_len, width)
    block_out = resid_mid + gate_two * mlp_out
    grad_gate_two = jnp.sum(cotangent * mlp_out, axis=1)
    grad_act = matmul(grad_mlp_low, fc2_full).reshape(fc1_pre.shape)
    slope = 0.5 * (1.0 + tanh_inner) + 0.5 * fc1_pre * (
        1.0 - tanh_inner * tanh_inner
    ) * gelu_scale * (1.0 + 3.0 * gelu_cubic * fc1_pre * fc1_pre)
    grad_pre = grad_act * slope
    grad_pre_low = flat_rows(grad_pre.astype(bf16))
    grad_fc1_bias = jnp.sum(flat_rows(grad_pre), axis=0)
    grad_fc1 = by_owner(matmul_tn(grad_pre_low, flat_rows(hidden_two)))
    grad_fc1, grad_pre_low = tie(grad_fc1, grad_pre_low)
    half_fc1 = start_reduce(cube, grad_fc1)
    grad_hidden_two = matmul(grad_pre_low, fc1_full).reshape(count, seq_len, width)
    grad_shift_two = jnp.sum(grad_hidden_two, axis=1)
    grad_scale_two = jnp.sum(grad_hidden_two * normed_two, axis=1)
    grad_mid = cotangent + norm_back(grad_hidden_two * (1.0 + scale_two), normed_two, inv_two)
    grad_gate_one = jnp.sum(grad_mid * attn_out, axis=1)
    grad_attn = grad_mid * gate_one
    grad_attn_low = flat_rows(grad_attn.astype(bf16))
    grad_proj_bias = jnp.sum(flat_rows(grad_attn), axis=0)
    grad_proj = by_owner(matmul_tn(grad_attn_low, flat_rows(attended)))
    grad_proj, grad_attn_low = tie(grad_proj, grad_attn_low)
    half_proj = start_reduce(cube, grad_proj)
    grad_attended = matmul(grad_attn_low, proj_full).astype(bf16).reshape(head_shape)
    part_both = reduce_rep(cube, [half_proj, half_fc1])
    scores = head_product("lqhd,lkhd->lhqk", query_heads, key_heads) * scale
    prob_full = jnp.exp(scores - log_total)
    prob_low = prob_full.astype(bf16)
    grad_value = head_product("lhqk,lqhd->lkhd", prob_low, grad_attended).reshape(
        count * seq_len, width
    )
    grad_prob = head_product("lqhd,lkhd->lhqk", grad_attended, value_heads)
    row_delta = jnp.sum(prob_full * grad_prob, axis=-1, keepdims=True)
    grad_scores = (prob_full * (grad_prob - row_delta) * scale).astype(bf16)
    grad_query = head_product("lhqk,lkhd->lqhd", grad_scores, key_heads).reshape(
        count * seq_len, width
    )
    grad_key = head_product("lhqk,lqhd->lkhd", grad_scores, query_heads).reshape(
        count * seq_len, width
    )
    grad_query_bias = jnp.sum(grad_query, axis=0)
    grad_value_bias = jnp.sum(grad_value, axis=0)
    grad_qkv_low = jnp.concatenate([grad_query, grad_key, grad_value], axis=1).astype(bf16)
    grad_qkv_low, part_fc2 = tie(grad_qkv_low, part_fc2)
    sum_fc2 = reduce_shard(cube, part_fc2)
    grad_qkv = by_owner(matmul_tn(grad_qkv_low, flat_rows(hidden_one)))
    grad_qkv, grad_qkv_low = tie(grad_qkv, grad_qkv_low)
    half_qkv = start_reduce(cube, grad_qkv)
    grad_hidden_one = matmul(grad_qkv_low, qkv_full).reshape(count, seq_len, width)
    grad_shift_one = jnp.sum(grad_hidden_one, axis=1)
    grad_scale_one = jnp.sum(grad_hidden_one * normed_one, axis=1)
    grad_input = grad_mid + norm_back(grad_hidden_one * (1.0 + scale_one), normed_one, inv_one)
    grad_mod = jnp.concatenate(
        [grad_shift_one, grad_scale_one, grad_gate_one, grad_shift_two, grad_scale_two, grad_gate_two],
        axis=1,
    )
    biases = (grad_query_bias, grad_value_bias, grad_proj_bias, grad_fc1_bias, grad_fc2_bias)
    part_qkv = reduce_rep(cube, [half_qkv])
    sum_both = reduce_shard(cube, part_both)
    sum_qkv = reduce_shard(cube, part_qkv)

    early = spread_parts(cube, jnp.concatenate([sum_fc2, sum_both], axis=0))
    late = spread_parts(cube, sum_qkv)
    sizes = [sum_fc2.shape[0], grad_proj.shape[2]]
    fc2_low, proj_low, fc1_low = jnp.split(early, [sizes[0], sizes[0] + sizes[1]], axis=1)
    out_qkv = late.reshape(-1, width).T.astype(f32)
    out_proj = proj_low.reshape(-1, width).T.astype(f32)
    out_fc1 = fc1_low.reshape(-1, width).T.astype(f32)
    out_fc2 = jnp.swapaxes(fc2_low.reshape(blocks, outs, width), 1, 2).reshape(blocks * width, outs)
    out_fc2 = out_fc2.astype(f32)

    per_owner = [grad_mod.reshape(count, n_shard, wide).swapaxes(0, 1).reshape(n_shard, count * wide)]
    per_owner += [b.reshape(n_shard, -1) for b in biases]
    rows = reorder(jnp.concatenate(per_owner, axis=1), cube.shard, cube.shard_bits)
    rows = small_exchange(cube, rows)
    grad_rows = rows[:, : count * wide].reshape(n_shard * count, wide)
    cond_rows = cond_group.reshape(n_shard, count * width).astype(f32)
    all_rows = small_gather_rep(cube, jnp.concatenate([rows, cond_rows], axis=1))
    all_rows = reorder(all_rows.reshape(n_rep, n_shard, -1), cube.rep, cube.rep_bits)
    all_rows, all_cond = all_rows[:, :, : rows.shape[1]], all_rows[:, :, rows.shape[1] :]
    all_cond = all_cond.astype(bf16).reshape(-1, width)
    mod_all = all_rows[:, :, : count * wide].reshape(-1, wide)
    out_ada = matmul_tn(all_cond, mod_all.astype(bf16))
    out_ada_bias = jnp.sum(mod_all, axis=0)
    sums = jnp.sum(all_rows[:, :, count * wide :].reshape(n_rep * n_shard, -1), axis=0)
    out_q, out_v, out_p, out_f1, out_f2 = jnp.split(sums, ends)
    cond_part = matmul_nt(grad_rows.astype(bf16), ada_weight).reshape(n_shard, count, width)
    grad_cond_row = small_scatter_sum(cube, cond_part)[0]
    grad_cond = grad_cond_row * sigmoid_c * (1.0 + conditioning * (1.0 - sigmoid_c))
    return (
        block_out,
        grad_input,
        grad_cond,
        out_ada,
        out_ada_bias,
        out_qkv,
        out_q,
        out_v,
        out_proj,
        out_p,
        out_fc1,
        out_f1,
        out_fc2,
        out_f2,
    )


def solution(mesh):
    def local(*args):
        return local_step(Cube(mesh.shape["rep"], mesh.shape["shard"]), *args)

    placed = (
        P(("rep", "shard"), None, None),
        P(("rep", "shard"), None),
        P(("rep", "shard"), None, None),
        P(None, "shard"),
        P("shard"),
        P(None, "shard"),
        P("shard"),
        P("shard"),
        P(None, "shard"),
        P("shard"),
        P(None, "shard"),
        P("shard"),
        P(None, "shard"),
        P("shard"),
    )
    return jax.shard_map(
        local,
        mesh=mesh,
        in_specs=placed,
        out_specs=placed[:1] + placed[:2] + placed[3:],
        check_vma=False,
    )
```
